32 devices in a mesh: shard: 16 (over z, y, x), rep: 2 (over core).
Axes of the slice: x: 2, y: 2, z: 4, core: 2. Of those that a mesh axis runs over, the one named last changes fastest.
Arguments:
- dense_feats: bfloat16 [4096, 13], P(('shard', 'rep')), may hold values from -6 to 6
- lookup_ids: int32 [4096, 13, 4], P(('shard', 'rep')), may hold values from 0 to 1023, as said below
- bag_lengths: int32 [4096, 13], P(('shard', 'rep')), may hold values from 1 to 4
- bottom_w1: bfloat16 [13, 512], replicated, may hold values from -1.75 to 1.75
- bottom_w2: bfloat16 [512, 256], replicated, may hold values from -0.25 to 0.25
- bottom_w3: bfloat16 [256, 128], replicated, may hold values from -0.375 to 0.375
- tables: bfloat16 [13, 1024, 128], P(None, 'shard'), may hold values from -3 to 3
- accum: float32 [13, 1024], P(None, 'shard'), may hold values from 0.05 to 1
- cross_down: bfloat16 [1792, 512], replicated, may hold values from -0.125 to 0.125
- cross_up: bfloat16 [512, 1792], replicated, may hold values from -0.25 to 0.25
- cross_bias: float32 [1792], replicated, may hold values from -3 to 3
- cotangent: bfloat16 [4096, 1792], P(('shard', 'rep')), may hold values from -0.3984375 to 0.3984375
Outputs:
- crossed: bfloat16 [4096, 1792], P(('shard', 'rep'))
- new_tables: float32 [13, 1024, 128], P(None, 'shard')
- new_accum: float32 [13, 1024], P(None, 'shard')
The draws below stay inside these ranges and needn't reach their ends.
Inputs may be any that keep to these rules, and one draw needn't show every extreme that they name: `lookup_ids`: row r of a table is held by index r // 64 of shard. Among the 6656 slots of one device (used or not), at most 624 name rows held by any one index of shard, and in every draw one index of shard gets exactly 624 from every device. Only the first bag_lengths[s, t] slots of bag (s, t) are used.
All inputs are finite; a program needn't handle non-finite values.
Results may differ from the reference program's by a relative error of at most 0.0065.
Values may be sent and summed in bfloat16 or wider, within the bound.
A program may use at most 128 MiB of HBM per device.

```python
import math
import jax
import jax.numpy as jnp
from jax import lax

EMB = 128
NT = 13
DENSE = 13
H1 = 512
H2 = 256
RANK = 512
POOL = 4
B_DEV = 128
ROWS_DEV = 64
X = 1792
SAMPLES = 4096
ROWS = 1024
N_SHARD = 16
N_REP = 2


def draw_lookup_ids(key, part):
    block_count = N_SHARD * N_REP
    slot_count = B_DEV * NT * POOL
    mean_load = slot_count // N_SHARD
    half_load = mean_load // 2
    pair_count = N_SHARD // 2
    hot_key, rest_key = jax.random.split(jax.random.fold_in(key, 11))
    hottest = jax.random.randint(hot_key, (), 0, N_SHARD)

    def one_block(block_key):
        extra_key, label_key, shuffle_key, row_key = jax.random.split(block_key, 4)
        extra_load = jax.random.randint(extra_key, (pair_count,), 0, half_load + 1).at[0].set(half_load)
        counts = jnp.concatenate([mean_load + extra_load, mean_load - extra_load])
        labels = jax.random.permutation(label_key, N_SHARD)
        owner_of = (labels - labels[0] + hottest) % N_SHARD
        bounds = jnp.cumsum(counts)
        virtual = jnp.searchsorted(bounds, jnp.arange(slot_count), side='right')
        owners = jax.random.permutation(shuffle_key, owner_of[virtual])
        within_rows = jax.random.randint(row_key, (slot_count,), 0, ROWS_DEV)
        return (owners * ROWS_DEV + within_rows).reshape(B_DEV, NT, POOL)
    block_keys = jax.random.split(rest_key, block_count)
    return jax.vmap(one_block)(block_keys).reshape(B_DEV * block_count, NT, POOL).astype(jnp.int32)


def with_ends(drawn, rng, least, top_value):
    index_at = [jax.random.randint(jax.random.fold_in(rng, axis), (), 0, length) for axis, length in enumerate(drawn.shape)]
    longest = drawn.shape.index(max(drawn.shape))
    beside = index_at[:longest] + [(index_at[longest] + 1) % drawn.shape[longest]] + index_at[longest + 1:]
    return drawn.at[tuple(index_at)].set(least).at[tuple(beside)].set(top_value)


def levels(stream_key, shape, cuts, least, high):
    def one(position, parts):
        draws = jax.random.uniform(jax.random.fold_in(jax.random.fold_in(stream_key, 6), position), (parts,), jnp.float32, least / len(cuts), high / len(cuts))
        return jnp.repeat(jnp.exp(draws), shape[position] // parts).reshape((-1,) + (1,) * (len(shape) - position - 1))

    loudness = one(*cuts[0])
    for cut in cuts[1:]:
        loudness = loudness * one(*cut)
    return loudness


def noise(rng, extent, deviation, reach, cuts=(), kind=jnp.bfloat16):
    array = deviation * jax.random.normal(rng, extent, jnp.float32)
    if cuts:
        array = array * levels(rng, extent, cuts, -0.22, 0.18)
    return jnp.clip(array, -reach, reach).astype(kind)


def setup_inputs(seed: int = 0) -> dict:
    key_list = jax.random.split(jax.random.key(seed), 13)
    dense_feats = noise(key_list[0], (SAMPLES, DENSE), 1.0, 6.0, ((0, 32),))
    lookup_ids = draw_lookup_ids(jax.random.fold_in(key_list[12], 71), 0)
    bag_lengths = with_ends(jax.random.randint(key_list[2], (SAMPLES, NT), 1, POOL + 1), jax.random.fold_in(key_list[2], 1), 1, POOL).astype(jnp.int32)
    bottom_w1 = noise(key_list[3], (DENSE, H1), DENSE ** -0.5, 1.75)
    bottom_w2 = noise(key_list[4], (H1, H2), H1 ** -0.5, 0.25)
    bottom_w3 = noise(key_list[5], (H2, EMB), H2 ** -0.5, 0.375)
    tables = noise(key_list[6], (NT, ROWS, EMB), 0.5, 3.0, ((1, 16),))
    accum = jnp.clip(jnp.exp(math.log(1.0) - 2.9957323 * jax.random.uniform(key_list[7], (NT, ROWS), jnp.float32) ** levels(key_list[7], (NT, ROWS), ((1, 16),), -0.2, 0.2)), 0.05, 1.0)
    cross_down = noise(key_list[8], (X, RANK), X ** -0.5, 0.125)
    cross_up = noise(key_list[9], (RANK, X), RANK ** -0.5, 0.25)
    cross_bias = noise(key_list[10], (X,), 0.5, 3.0, (), jnp.float32)
    cotangent = noise(key_list[11], (SAMPLES, X), 0.05, 0.3984375, ((0, 32),))
    return dict(dense_feats=dense_feats, lookup_ids=lookup_ids, bag_lengths=bag_lengths, bottom_w1=bottom_w1, bottom_w2=bottom_w2, bottom_w3=bottom_w3, tables=tables, accum=accum, cross_down=cross_down, cross_up=cross_up, cross_bias=cross_bias, cotangent=cotangent)


step_size = 1.0
adagrad_eps = 1e-08

def cross_block(stacked, cross_down, cross_up, cross_bias, cotangent):
    low_rank = jnp.dot(stacked, cross_down, preferred_element_type=jnp.float32).astype(jnp.bfloat16)
    cross_hidden = jnp.dot(low_rank, cross_up, preferred_element_type=jnp.float32)
    widened = stacked.astype(jnp.float32)
    crossed = (widened * (cross_hidden + cross_bias) + widened).astype(jnp.bfloat16)
    cot_wide = cotangent.astype(jnp.float32)
    hidden_grad = (cot_wide * widened).astype(jnp.bfloat16)
    low_grad = jnp.dot(hidden_grad, cross_up.T, preferred_element_type=jnp.float32).astype(jnp.bfloat16)
    input_grad = cot_wide * (cross_hidden + cross_bias + 1.0) + jnp.dot(low_grad, cross_down.T, preferred_element_type=jnp.float32)
    return (crossed, input_grad)

def reference(dense_feats, lookup_ids, bag_lengths, bottom_w1, bottom_w2, bottom_w3, tables, accum, cross_down, cross_up, cross_bias, cotangent):
    blocks = N_SHARD * N_REP
    table_rows_flat = tables.reshape(NT * ROWS, EMB)
    offsets = (jnp.arange(NT, dtype=jnp.int32) * ROWS)[None, :, None]
    slot_index = jnp.arange(POOL, dtype=jnp.int32)[None, None, :]

    def one_block(running_total, piece_list):
        dense_slice, id_part, length_part, cot_part, block_index = piece_list
        live_mask = (slot_index < length_part[:, :, None]).astype(jnp.float32)
        flat_ids = (id_part + offsets).astype(jnp.int32)
        looked = table_rows_flat[flat_ids].astype(jnp.float32) * live_mask[..., None]
        pooled = lax.optimization_barrier(jnp.sum(looked, axis=2))
        first_layer = jax.nn.relu(jnp.dot(dense_slice, bottom_w1, preferred_element_type=jnp.float32)).astype(jnp.bfloat16)
        second_layer = jax.nn.relu(jnp.dot(first_layer, bottom_w2, preferred_element_type=jnp.float32)).astype(jnp.bfloat16)
        third_layer = jax.nn.relu(jnp.dot(second_layer, bottom_w3, preferred_element_type=jnp.float32)).astype(jnp.bfloat16)
        stacked = jnp.concatenate([third_layer, pooled.reshape(B_DEV, NT * EMB).astype(jnp.bfloat16)], axis=1)
        crossed, input_grad = cross_block(stacked, cross_down, cross_up, cross_bias, cot_part)
        pooled_grad = input_grad[:, EMB:].astype(jnp.bfloat16).reshape(B_DEV, NT, 1, EMB)
        entry_grad = pooled_grad.astype(jnp.float32) * live_mask[..., None]
        group_index = block_index % N_REP
        running_total = running_total.at[group_index, flat_ids.reshape(-1)].add(entry_grad.reshape(-1, EMB))
        return (running_total, crossed)
    piece_list = (dense_feats.reshape(blocks, B_DEV, DENSE), lookup_ids.reshape(blocks, B_DEV, NT, POOL), bag_lengths.reshape(blocks, B_DEV, NT), cotangent.reshape(blocks, B_DEV, X), jnp.arange(blocks, dtype=jnp.int32))
    initial = jnp.zeros((N_REP, NT * ROWS, EMB), jnp.float32)
    summed, crossed = lax.scan(one_block, initial, piece_list)
    rounded = lax.optimization_barrier(summed.astype(jnp.bfloat16)).astype(jnp.float32)
    row_grad = lax.optimization_barrier(jnp.sum(rounded, axis=0))
    new_accum = accum.reshape(-1) + lax.optimization_barrier(jnp.mean(row_grad * row_grad, axis=1))
    new_tables = table_rows_flat.astype(jnp.float32) - step_size * row_grad / (jnp.sqrt(new_accum)[:, None] + adagrad_eps)
    return (crossed.reshape(SAMPLES, X), new_tables.reshape(NT, ROWS, EMB), new_accum.reshape(NT, ROWS))
```

```python
import functools

import jax
import jax.numpy as jnp
from jax import lax
from jax.experimental import pallas as pl
from jax.experimental.pallas import tpu as pltpu
from jax.sharding import PartitionSpec as P

step_size = 1.0
adagrad_eps = 1e-08
contract_last = (((1,), (1,)), ((), ()))


def step_kernel(
    table_count,
    emb_width,
    id_columns,
    id_rows,
    table_block,
    dense,
    w1,
    w2,
    w3,
    cross_down,
    cross_up,
    cross_bias,
    cotangent,
    crossed,
    partial,
    stacked,
    pooled_grad,
):
    step = pl.program_id(0)
    shards, _, rows_dev, _ = table_block.shape
    samples, features = cotangent.shape
    pool_slots = id_columns.shape[2]
    group = min(shards, 16)
    chunk = group * rows_dev

    @pl.when(step < table_count)
    def _lookup():
        ids = id_columns[0]
        total = jnp.zeros((samples, emb_width), jnp.float32)
        for first in range(0, shards, group):
            names = lax.broadcasted_iota(jnp.int32, (samples, chunk), 1) + first * rows_dev
            counts = jnp.zeros((samples, chunk), jnp.float32)
            for slot in range(pool_slots):
                counts = counts + jnp.where(names == ids[:, slot : slot + 1], 1.0, 0.0)
            rows = table_block[first : first + group, 0].reshape(chunk, emb_width)
            total = total + jnp.dot(
                counts.astype(jnp.bfloat16), rows, preferred_element_type=jnp.float32
            )
        place = pl.multiple_of((step + 1) * emb_width, emb_width)
        stacked[:, pl.ds(place, emb_width)] = total.astype(jnp.bfloat16)

    @pl.when(step == table_count - 1)
    def _cross():
        def layer(x, w):
            return jax.nn.relu(jnp.dot(x, w[...], preferred_element_type=jnp.float32)).astype(
                jnp.bfloat16
            )

        stacked[:, :emb_width] = layer(layer(layer(dense[...], w1), w2), w3)
        low_rank = jnp.dot(
            stacked[...], cross_down[...], preferred_element_type=jnp.float32
        ).astype(jnp.bfloat16)
        hidden_grad = (
            cotangent[...].astype(jnp.float32) * stacked[...].astype(jnp.float32)
        ).astype(jnp.bfloat16)
        low_grad = lax.dot_general(
            hidden_grad, cross_up[...], contract_last, preferred_element_type=jnp.float32
        ).astype(jnp.bfloat16)
        width = 2 * emb_width if features % (2 * emb_width) == 0 else emb_width
        for start in range(0, features, width):
            part = slice(start, start + width)
            hidden = (
                jnp.dot(low_rank, cross_up[:, part], preferred_element_type=jnp.float32)
                + cross_bias[:, part]
            )
            wide = stacked[:, part].astype(jnp.float32)
            crossed[:, part] = (wide * hidden + wide).astype(jnp.bfloat16)
            back = lax.dot_general(
                low_grad, cross_down[part, :], contract_last, preferred_element_type=jnp.float32
            )
            grad = cotangent[:, part].astype(jnp.float32) * (hidden + 1.0) + back
            for inner in range(0, width, emb_width):
                table = (start + inner) // emb_width - 1
                if table >= 0:
                    pooled_grad[table] = grad[:, inner : inner + emb_width].astype(jnp.bfloat16)

    @pl.when(step >= table_count)
    def _spread():
        ids = id_rows[0]
        grad = pooled_grad[step - table_count]
        for first in range(0, shards, group):
            names = lax.broadcasted_iota(jnp.int32, (chunk, samples), 0) + first * rows_dev
            counts = jnp.zeros((chunk, samples), jnp.float32)
            for slot in range(pool_slots):
                counts = counts + jnp.where(names == ids[slot : slot + 1, :], 1.0, 0.0)
            sums = jnp.dot(counts.astype(jnp.bfloat16), grad, preferred_element_type=jnp.float32)
            partial[first : first + group, 0] = sums.astype(jnp.bfloat16).reshape(
                group, rows_dev, emb_width
            )


def per_device(
    dense_feats,
    lookup_ids,
    bag_lengths,
    bottom_w1,
    bottom_w2,
    bottom_w3,
    tables,
    accum,
    cross_down,
    cross_up,
    cross_bias,
    cotangent,
):
    shards = lax.axis_size("shard")
    reps = lax.axis_size("rep")
    samples, table_count, pool_slots = lookup_ids.shape
    rows_dev, emb_width = tables.shape[1:]
    features = cotangent.shape[1]
    gathered = lax.all_gather(tables, "shard", axis=0, tiled=False)
    live_mask = jnp.arange(pool_slots, dtype=jnp.int32)[None, None, :] < bag_lengths[:, :, None]
    coded = jnp.where(live_mask, lookup_ids, -1)
    id_columns = coded.transpose(1, 0, 2)
    id_rows = coded.transpose(1, 2, 0)

    def whole(array):
        return pl.BlockSpec(array.shape, lambda i: (0,) * array.ndim)

    bias = cross_bias[None, :]
    last = table_count - 1
    crossed, partial = pl.pallas_call(
        functools.partial(step_kernel, table_count, emb_width),
        grid=(2 * table_count,),
        in_specs=[
            pl.BlockSpec((1, samples, pool_slots), lambda i: (jnp.minimum(i, last), 0, 0)),
            pl.BlockSpec(
                (1, pool_slots, samples), lambda i: (jnp.maximum(i - table_count, 0), 0, 0)
            ),
            pl.BlockSpec(
                (shards, 1, rows_dev, emb_width), lambda i: (0, jnp.minimum(i, last), 0, 0)
            ),
            whole(dense_feats),
            whole(bottom_w1),
            whole(bottom_w2),
            whole(bottom_w3),
            whole(cross_down),
            whole(cross_up),
            whole(bias),
            whole(cotangent),
        ],
        out_specs=[
            pl.BlockSpec((samples, features), lambda i: (0, 0)),
            pl.BlockSpec(
                (shards, 1, rows_dev, emb_width),
                lambda i: (0, jnp.maximum(i - table_count, 0), 0, 0),
            ),
        ],
        out_shape=[
            jax.ShapeDtypeStruct((samples, features), jnp.bfloat16),
            jax.ShapeDtypeStruct((shards, table_count, rows_dev, emb_width), jnp.bfloat16),
        ],
        scratch_shapes=[
            pltpu.VMEM((samples, features), jnp.bfloat16),
            pltpu.VMEM((table_count, samples, emb_width), jnp.bfloat16),
        ],
        compiler_params=pltpu.CompilerParams(
            dimension_semantics=("arbitrary",), vmem_limit_bytes=40 * 2**20
        ),
    )(
        id_columns,
        id_rows,
        gathered,
        dense_feats,
        bottom_w1,
        bottom_w2,
        bottom_w3,
        cross_down,
        cross_up,
        bias,
        cotangent,
    )
    received = lax.all_to_all(partial, "shard", split_axis=0, concat_axis=0, tiled=True)
    group_grad = jnp.sum(received.astype(jnp.float32), axis=0).astype(jnp.bfloat16)
    row_grad = group_grad.astype(jnp.float32)
    shifted = group_grad
    for _ in range(reps - 1):
        shifted = lax.ppermute(shifted, "rep", [(r, (r + 1) % reps) for r in range(reps)])
        row_grad = row_grad + shifted.astype(jnp.float32)
    new_accum = accum + jnp.mean(row_grad * row_grad, axis=2)
    new_tables = tables.astype(jnp.float32) - step_size * row_grad / (
        jnp.sqrt(new_accum)[:, :, None] + adagrad_eps
    )
    return (crossed, new_tables, new_accum)


def solution(mesh):
    in_specs = (
        P(("shard", "rep"), None),
        P(("shard", "rep"), None, None),
        P(("shard", "rep"), None),
        P(),
        P(),
        P(),
        P(None, "shard", None),
        P(None, "shard"),
        P(),
        P(),
        P(),
        P(("shard", "rep"), None),
    )
    out_specs = (P(("shard", "rep"), None), P(None, "shard", None), P(None, "shard"))
    return jax.shard_map(
        per_device, mesh=mesh, in_specs=in_specs, out_specs=out_specs, check_vma=False
    )
```

```python
import functools

import jax
import jax.numpy as jnp
from jax import lax
from jax.experimental import pallas as pl
from jax.experimental.pallas import tpu as pltpu
from jax.sharding import PartitionSpec as P

step_size = 1.0
adagrad_eps = 1e-08
contract_last = (((1,), (1,)), ((), ()))


def step_kernel(
    table_count,
    emb_width,
    reps,
    id_columns,
    id_rows,
    dense,
    w1,
    w2,
    w3,
    cross_down,
    cross_up,
    cross_bias,
    cotangent,
    *refs,
):
    table_blocks, (crossed, *partials) = refs[:reps], refs[reps : 2 * reps + 1]
    stacked, pooled_grad = refs[2 * reps + 1 :]
    step = pl.program_id(0)
    shards, _, rows_dev, _ = table_blocks[0].shape
    pieces = [(turn, first) for turn in range(reps) for first in range(0, shards, min(shards, 16))]
    samples, features = cotangent.shape
    pool_slots = id_columns.shape[2]
    group = min(shards, 16)
    chunk = group * rows_dev

    @pl.when(step < table_count)
    def _lookup():
        ids = id_columns[0]
        total = jnp.zeros((samples, emb_width), jnp.float32)
        for turn, first in pieces:
            begin = (turn * shards + first) * rows_dev
            names = lax.broadcasted_iota(jnp.int32, (samples, chunk), 1) + begin
            counts = jnp.zeros((samples, chunk), jnp.float32)
            for slot in range(pool_slots):
                counts = counts + jnp.where(names == ids[:, slot : slot + 1], 1.0, 0.0)
            rows = table_blocks[turn][first : first + group, 0].reshape(chunk, emb_width)
            total = total + jnp.dot(
                counts.astype(jnp.bfloat16), rows, preferred_element_type=jnp.float32
            )
        place = pl.multiple_of((step + 1) * emb_width, emb_width)
        stacked[:, pl.ds(place, emb_width)] = total.astype(jnp.bfloat16)

    @pl.when(step == table_count - 1)
    def _cross():
        def layer(x, w):
            return jax.nn.relu(jnp.dot(x, w[...], preferred_element_type=jnp.float32)).astype(
                jnp.bfloat16
            )

        stacked[:, :emb_width] = layer(layer(layer(dense[...], w1), w2), w3)
        low_rank = jnp.dot(
            stacked[...], cross_down[...], preferred_element_type=jnp.float32
        ).astype(jnp.bfloat16)
        hidden_grad = (
            cotangent[...].astype(jnp.float32) * stacked[...].astype(jnp.float32)
        ).astype(jnp.bfloat16)
        low_grad = lax.dot_general(
            hidden_grad, cross_up[...], contract_last, preferred_element_type=jnp.float32
        ).astype(jnp.bfloat16)
        width = 2 * emb_width if features % (2 * emb_width) == 0 else emb_width
        for start in range(0, features, width):
            part = slice(start, start + width)
            hidden = (
                jnp.dot(low_rank, cross_up[:, part], preferred_element_type=jnp.float32)
                + cross_bias[:, part]
            )
            wide = stacked[:, part].astype(jnp.float32)
            crossed[:, part] = (wide * hidden + wide).astype(jnp.bfloat16)
            back = lax.dot_general(
                low_grad, cross_down[part, :], contract_last, preferred_element_type=jnp.float32
            )
            grad = cotangent[:, part].astype(jnp.float32) * (hidden + 1.0) + back
            for inner in range(0, width, emb_width):
                table = (start + inner) // emb_width - 1
                if table >= 0:
                    pooled_grad[table] = grad[:, inner : inner + emb_width].astype(jnp.bfloat16)

    @pl.when(step >= table_count)
    def _spread():
        ids = id_rows[0]
        grad = pooled_grad[step - table_count]
        for turn, first in pieces:
            begin = (turn * shards + first) * rows_dev
            names = lax.broadcasted_iota(jnp.int32, (chunk, samples), 0) + begin
            counts = jnp.zeros((chunk, samples), jnp.float32)
            for slot in range(pool_slots):
                counts = counts + jnp.where(names == ids[slot : slot + 1, :], 1.0, 0.0)
            sums = jnp.dot(counts.astype(jnp.bfloat16), grad, preferred_element_type=jnp.float32)
            partials[turn][first : first + group, 0] = sums.astype(jnp.bfloat16).reshape(
                group, rows_dev, emb_width
            )


def per_device(
    dense_feats,
    lookup_ids,
    bag_lengths,
    bottom_w1,
    bottom_w2,
    bottom_w3,
    tables,
    accum,
    cross_down,
    cross_up,
    cross_bias,
    cotangent,
):
    shards = lax.axis_size("shard")
    reps = lax.axis_size("rep")
    samples, table_count, pool_slots = lookup_ids.shape
    rows_dev, emb_width = tables.shape[1:]
    features = cotangent.shape[1]
    me = lax.axis_index("rep")
    half = rows_dev // reps

    def shift(array, by):
        return lax.ppermute(array, "rep", [(r, (r + by) % reps) for r in range(reps)])

    own_rows = lax.dynamic_slice_in_dim(tables, me * half, half, axis=1)
    own_gathered = lax.all_gather(own_rows, "shard", axis=0, tiled=False)
    gathered = [own_gathered] + [shift(own_gathered, -turn) for turn in range(1, reps)]
    live_mask = jnp.arange(pool_slots, dtype=jnp.int32)[None, None, :] < bag_lengths[:, :, None]
    within = lookup_ids % rows_dev
    turns = (within // half - me + reps) % reps
    places = (turns * shards + lookup_ids // rows_dev) * half + within % half
    coded = jnp.where(live_mask, places, -1)
    id_columns = coded.transpose(1, 0, 2)
    id_rows = coded.transpose(1, 2, 0)

    def whole(array):
        return pl.BlockSpec(array.shape, lambda i: (0,) * array.ndim)

    bias = cross_bias[None, :]
    last = table_count - 1
    crossed, *partials = pl.pallas_call(
        functools.partial(step_kernel, table_count, emb_width, reps),
        grid=(2 * table_count,),
        in_specs=[
            pl.BlockSpec((1, samples, pool_slots), lambda i: (jnp.minimum(i, last), 0, 0)),
            pl.BlockSpec(
                (1, pool_slots, samples), lambda i: (jnp.maximum(i - table_count, 0), 0, 0)
            ),
            whole(dense_feats),
            whole(bottom_w1),
            whole(bottom_w2),
            whole(bottom_w3),
            whole(cross_down),
            whole(cross_up),
            whole(bias),
            whole(cotangent),
        ]
        + [pl.BlockSpec((shards, 1, half, emb_width), lambda i: (0, jnp.minimum(i, last), 0, 0))]
        * reps,
        out_specs=[
            pl.BlockSpec((samples, features), lambda i: (0, 0)),
        ]
        + [
            pl.BlockSpec(
                (shards, 1, half, emb_width),
                lambda i: (0, jnp.maximum(i - table_count, 0), 0, 0),
            )
        ]
        * reps,
        out_shape=[
            jax.ShapeDtypeStruct((samples, features), jnp.bfloat16),
        ]
        + [jax.ShapeDtypeStruct((shards, table_count, half, emb_width), jnp.bfloat16)] * reps,
        scratch_shapes=[
            pltpu.VMEM((samples, features), jnp.bfloat16),
            pltpu.VMEM((table_count, samples, emb_width), jnp.bfloat16),
        ],
        compiler_params=pltpu.CompilerParams(
            dimension_semantics=("arbitrary",), vmem_limit_bytes=40 * 2**20
        ),
    )(
        id_columns,
        id_rows,
        dense_feats,
        bottom_w1,
        bottom_w2,
        bottom_w3,
        cross_down,
        cross_up,
        bias,
        cotangent,
        *gathered,
    )
    chip_sum = partials[0].astype(jnp.float32)
    for turn in range(1, reps):
        chip_sum = chip_sum + shift(partials[turn], turn).astype(jnp.float32)
    received = lax.all_to_all(
        chip_sum.astype(jnp.bfloat16), "shard", split_axis=0, concat_axis=0, tiled=True
    )
    own_grad = jnp.sum(received.astype(jnp.float32), axis=0)
    row_grad = jnp.zeros((table_count, rows_dev, emb_width), jnp.float32)
    for turn in range(reps):
        piece = shift(own_grad, -turn) if turn else own_grad
        row_grad = lax.dynamic_update_slice_in_dim(
            row_grad, piece, (me + turn) % reps * half, axis=1
        )
    new_accum = accum + jnp.mean(row_grad * row_grad, axis=2)
    new_tables = tables.astype(jnp.float32) - step_size * row_grad / (
        jnp.sqrt(new_accum)[:, :, None] + adagrad_eps
    )
    return (crossed, new_tables, new_accum)


def solution(mesh):
    in_specs = (
        P(("shard", "rep"), None),
        P(("shard", "rep"), None, None),
        P(("shard", "rep"), None),
        P(),
        P(),
        P(),
        P(None, "shard", None),
        P(None, "shard"),
        P(),
        P(),
        P(),
        P(("shard", "rep"), None),
    )
    out_specs = (P(("shard", "rep"), None), P(None, "shard", None), P(None, "shard"))
    return jax.shard_map(
        per_device, mesh=mesh, in_specs=in_specs, out_specs=out_specs, check_vma=False
    )
```
